256 devices in a mesh: grp: 16 (over x_lo, z), blk: 16 (over x_hi, y, core).
Axes of the slice: x: 4 (x_hi: 2, x_lo: 2; x = x_hi * 2 + x_lo), y: 4, z: 8, core: 2. Of those that a mesh axis runs over, the one named last changes fastest.
Arguments:
- raw_ints: bfloat16 [2048, 256, 512], P('grp', 'blk'), may hold values from -0.59765625 to 0.59765625
- metric: bfloat16 [2048, 2048], P(None, 'grp'), as said below
- occ_energy: float32 [256], replicated, may hold values from -2 to -0.3
- virt_energy: float32 [512], replicated, may hold values from 0.2 to 5
Outputs:
- density: float32 [2048, 256, 512], P(None, ('blk', 'grp'))
- pair_energy: float32 [256, 4], P(('blk', 'grp'))
The draws below stay inside these ranges and needn't reach their ends.
Inputs may be any that keep to these rules, and one draw needn't show every extreme that they name: `metric`: Symmetric.
All inputs are finite; a program needn't handle non-finite values.
Results may differ from the reference program's by a relative error of at most 0.0033.
Values may be sent and summed in bfloat16 or wider, within the bound.
A program may use at most 128 MiB of HBM per device.

```python
import math
import jax
import jax.numpy as jnp
from jax import lax

NAUX = 2048
NV = 512
VISITS = 4
NOCC = 256
N_GRP = 16
N_BLK = 16


def draw_metric(key, part):
    first, second = jax.random.split(jax.random.fold_in(key, 7))
    noise = jax.random.normal(first, (NAUX, NAUX), jnp.float32)
    noise = (noise + noise.T) * (0.6 / jnp.sqrt(2.0 * NAUX))
    diag = 1.0 + 0.3 * jax.random.uniform(second, (NAUX,), jnp.float32)
    return (noise + jnp.diag(diag)).astype(jnp.bfloat16)


def block_scale(own_key, shape, cuts, low, largest):
    def one(axis_at, parts):
        steps = jax.random.uniform(jax.random.fold_in(jax.random.fold_in(own_key, 6), axis_at), (parts,), jnp.float32, low / len(cuts), largest / len(cuts))
        return jnp.repeat(jnp.exp(steps), shape[axis_at] // parts).reshape((-1,) + (1,) * (len(shape) - axis_at - 1))

    loudness = one(*cuts[0])
    for cut in cuts[1:]:
        loudness = loudness * one(*cut)
    return loudness


def bell_draw(stream_key, extent, scale, bound, shards=(), kind=jnp.bfloat16):
    drawn = scale * jax.random.normal(stream_key, extent, jnp.float32)
    if shards:
        drawn = drawn * block_scale(stream_key, extent, shards, -0.22, 0.18)
    return jnp.clip(drawn, -bound, bound).astype(kind)


def setup_inputs(seed: int = 0) -> dict:
    streams_of = jax.random.split(jax.random.key(seed), 5)
    return {
        "raw_ints": bell_draw(streams_of[0], (NAUX, NOCC, NV), 0.08, 0.59765625, ((0, 16), (1, 16))),
        "metric": draw_metric(jax.random.fold_in(streams_of[4], 71), 0),
        "occ_energy": jnp.clip(jax.random.uniform(streams_of[2], (NOCC,), jnp.float32, -2.0, -0.3), -2.0, -0.3),
        "virt_energy": jnp.clip(jnp.exp(jax.random.uniform(streams_of[3], (NV,), jnp.float32, math.log(0.2), math.log(5.0))), 0.2, 5.0),
    }


def chain_orbital(place):
    return (place % N_BLK) * N_GRP + place // N_BLK


def reference(raw_ints, metric, occ_energy, virt_energy):
    metric_wide = metric.astype(jnp.float32)

    def fit_one(orbital):
        block = lax.dynamic_index_in_dim(raw_ints, orbital, 1, keepdims=False).astype(jnp.float32)
        return jnp.dot(metric_wide, block, precision=lax.Precision.HIGHEST).astype(jnp.bfloat16)

    fitted = lax.map(fit_one, jnp.arange(NOCC, dtype=jnp.int32))

    def per_orbital(orbital):
        place = (orbital % N_GRP) * N_BLK + orbital // N_GRP
        own = lax.dynamic_index_in_dim(fitted, orbital, 0, keepdims=False).astype(jnp.float32)
        e_own = occ_energy[orbital]
        total = jnp.zeros((NAUX, NV), jnp.float32)
        energies = []
        for step in range(VISITS):
            if step == 0:
                partner = place
            else:
                partner = jnp.where((place - step) % 2 == 0, (place - step) % NOCC, (place + step) % NOCC)
            other_orb = chain_orbital(partner).astype(jnp.int32)
            other = lax.dynamic_index_in_dim(fitted, other_orb, 0, keepdims=False).astype(jnp.float32)
            coulomb = jnp.einsum("qa,qb->ab", own, other, precision=lax.Precision.HIGHEST)
            denom = e_own + occ_energy[other_orb] - virt_energy[:, None] - virt_energy[None, :]
            amplitude = coulomb / denom
            tilde = 2.0 * amplitude - amplitude.T
            energies.append(jnp.sum(coulomb * tilde))
            tilde_low = tilde.astype(jnp.bfloat16).astype(jnp.float32)
            total = total + jnp.einsum("qb,ab->qa", other, tilde_low, precision=lax.Precision.HIGHEST)
        return total, jnp.stack(energies)

    density, pair_energy = lax.map(per_orbital, jnp.arange(NOCC, dtype=jnp.int32))
    return jnp.transpose(density, (1, 0, 2)), pair_energy
```

```python
import functools

import jax
import jax.numpy as jnp
from jax import lax
from jax.experimental import pallas as pl
from jax.experimental.pallas import tpu as pltpu
from jax.sharding import PartitionSpec as P

VISITS = 4
NAUX = 2048
NV = 512
CHUNKS = 4
WIDE = NV // CHUNKS
MESH = pl.DeviceIdType.MESH
F32 = jnp.float32
BF16 = jnp.bfloat16


def device(xl, z, xh, y, c):
    return (xl * 8 + z, xh * 8 + y * 2 + c)


def kernel(
    raw, metric, occ, virt, out_hbm, energy_out,
    send, owned, full, mine, sib, near, far, mine_t, coul, amp, vsum, tlow, rows,
    a2a_s, a2a_r, m1_s, m1_r, mx_s, mx_r, my_s, my_r, xy_s, xy_r, yx_s, yx_r,
    sw_s, sw_r, sib_s, sib_r, vis_s, vis_r, far_s, far_r, out_s,
):
    g = lax.axis_index("grp")
    b = lax.axis_index("blk")
    xl, z = g // 8, g % 8
    xh, y, c = b // 8, (b // 2) % 4, b % 2
    x = xh * 2 + xl
    other = (g, b + 1 - 2 * c)
    chip = g * 8 + xh * 4 + y
    ahead = (chip + 1 - 2 * c) % 128
    behind = (chip + 127 + 2 * c) % 128

    def chip_core(n):
        return (n // 8, (n % 8) * 2 + c)

    def at_x(d):
        x2 = (x + d) % 4
        return device(x2 % 2, z, x2 // 2, y, c)

    def at_y(d):
        return device(xl, z, xh, (y + d) % 4, c)

    def at_g(d):
        return ((g + d) % 16, b)

    def at_z(d):
        return (xl * 8 + (z + d) % 8, b)

    barrier = pltpu.get_barrier_semaphore()
    partners = [at_g(d) for d in range(1, 16)]
    partners += [at_x(d) for d in range(1, 4)] + [at_y(d) for d in range(1, 4)]
    partners += [other, chip_core(ahead), chip_core(behind)]
    for partner in partners:
        pl.semaphore_signal(barrier, inc=1, device_id=partner, device_id_type=MESH)

    order = lax.broadcasted_iota(jnp.int32, (256, 256), 0)
    column = lax.broadcasted_iota(jnp.int32, (256, 256), 1)
    swap = jnp.where(column == (order % 16) * 16 + order // 16, 1.0, 0.0).astype(BF16)

    pl.semaphore_wait(barrier, len(partners))

    sends = []

    def push(src, dst, ssem, rsem, to):
        copy = pltpu.make_async_remote_copy(
            src_ref=src, dst_ref=dst, send_sem=ssem, recv_sem=rsem,
            device_id=to, device_id_type=MESH,
        )
        copy.start()
        sends.append(copy)

    def arrived(ref, sem):
        pltpu.make_async_copy(ref, ref, sem).wait()

    part = c * 8 + xh * 4 + y
    part_rows = pl.ds(pl.multiple_of(part * 128, 128), 128)
    own_columns = pl.ds(pl.multiple_of(g * 128, 128), 128)
    for d in range(1, 8):
        push(metric.at[part_rows, :], full.at[part_rows, own_columns], m1_s.at[d], m1_r, at_z(d))
    pltpu.make_async_copy(metric.at[part_rows, :], full.at[part_rows, own_columns], m1_r).start()

    def relayout(k, carry):
        at = pl.multiple_of(k * 256, 256)
        moved = jnp.dot(swap, raw[pl.ds(at, 256), :], preferred_element_type=F32).astype(BF16)
        to = pl.multiple_of(k * 16, 16)
        for i in range(16):
            send[i, pl.ds(to, 16), :] = moved[i * 16:(i + 1) * 16, :]
        return carry

    lax.fori_loop(0, 8, relayout, 0)

    land = pl.ds(pl.multiple_of(g * 128, 128), 128)
    for k in range(CHUNKS):
        cut = slice(k * WIDE, (k + 1) * WIDE)
        pltpu.make_async_copy(send.at[g, :, cut], owned.at[land, cut], a2a_r.at[k]).start()
        for d in range(1, 16):
            to = at_g(d)
            push(send.at[to[0], :, cut], owned.at[land, cut], a2a_s.at[k, d], a2a_r.at[k], to)

    def piece(px, py, half):
        hi, lo = px // 2, px % 2
        at = pl.multiple_of((c * 8 + hi * 4 + py) * 128, 128)
        col = pl.multiple_of(lo * 1024 + half * 512, 512)
        return full.at[pl.ds(at, 128), pl.ds(col, 512)]

    def from_x(d):
        return (x + 4 - d) % 4

    def from_y(d):
        return (y + 4 - d) % 4

    arrived(full.at[part_rows, pl.ds(0, 1024)], m1_r)
    for d in (1, 3, 2):
        push(piece(x, y, 0), piece(x, y, 0), mx_s.at[d], mx_r.at[d], at_x(d))
        push(piece(x, y, 1), piece(x, y, 1), my_s.at[d], my_r.at[d], at_y(d))
    for d in (1, 3, 2):
        push(piece(x, y, 0), piece(x, y, 0), xy_s.at[0, d], xy_r.at[d], at_y(d))
        push(piece(x, y, 1), piece(x, y, 1), yx_s.at[0, d], yx_r.at[d], at_x(d))
    for e in (1, 3, 2):
        arrived(piece(x, y, 0), mx_r.at[e])
        for d in (1, 3, 2):
            p = piece(from_x(e), y, 0)
            push(p, p, xy_s.at[e, d], xy_r.at[d], at_y(d))
        arrived(piece(x, y, 1), my_r.at[e])
        for d in (1, 3, 2):
            p = piece(x, from_y(e), 1)
            push(p, p, yx_s.at[e, d], yx_r.at[d], at_x(d))
    core_rows = pl.ds(pl.multiple_of(c * 1024, 1024), 1024)
    for d in (1, 3, 2):
        arrived(full.at[pl.ds(0, 512), pl.ds(0, 512)], xy_r.at[d])
    for lo in range(2):
        p = full.at[core_rows, pl.ds(lo * 1024, 512)]
        push(p, p, sw_s.at[lo], sw_r, other)
    for d in (1, 3, 2):
        arrived(full.at[pl.ds(0, 512), pl.ds(0, 512)], yx_r.at[d])
    for lo in range(2):
        p = full.at[core_rows, pl.ds(lo * 1024 + 512, 512)]
        push(p, p, sw_s.at[2 + lo], sw_r, other)

    wide = jnp.broadcast_to(virt[...], (512, 512))
    vsum[...] = wide + wide.T

    arrived(full.at[core_rows, :], sw_r)

    for k in range(CHUNKS):
        cut = slice(k * WIDE, (k + 1) * WIDE)
        arrived(owned.at[:, cut], a2a_r.at[k])

        def fit(q, carry, cut=cut):
            at = pl.ds(pl.multiple_of(q * 256, 256), 256)
            fitted = jnp.dot(full[at, :], owned[:, cut], preferred_element_type=F32)
            mine[at, cut] = fitted.astype(BF16)
            mine_t[cut, at] = fitted.T.astype(BF16)
            return carry

        lax.fori_loop(0, 8, fit, 0)
        push(mine.at[:, cut], near.at[:, cut], vis_s.at[k], vis_r.at[k], chip_core(ahead))
        push(mine.at[:, cut], sib.at[:, cut], sib_s.at[k], sib_r.at[k], other)

    def orbital(p):
        return (p % 16) * 16 + p // 16

    place = g * 16 + b
    e_own = occ[orbital(place)]

    def partner(s):
        if s == 0:
            return place
        even = (place + 256 - s) % 2 == 0
        return jnp.where(even, place + 256 - s, place + s) % 256

    energies = []

    def terms(s, fit_of):
        e_sum = e_own + occ[orbital(partner(s))]

        def product(r, carry):
            at = pl.ds(pl.multiple_of(r * 128, 128), 128)
            value = jnp.dot(mine_t[at, :], fit_of[...], preferred_element_type=F32)
            coul[at, :] = value
            amp[at, :] = value / (e_sum - vsum[at, :])
            return carry

        lax.fori_loop(0, 4, product, 0)

        total = jnp.zeros((128, 512), F32)
        for r in range(4):
            at = slice(r * 128, (r + 1) * 128)
            straight = amp[at, :]
            turned = amp[:, at].T
            total = total + coul[at, :] * (2.0 * straight - turned)
            tlow[s * 512 + r * 128:s * 512 + (r + 1) * 128, :] = (
                2.0 * turned - straight
            ).astype(BF16)
        energies.append(jnp.sum(total))

    terms(0, mine)
    for k in range(CHUNKS):
        cut = slice(k * WIDE, (k + 1) * WIDE)
        arrived(near.at[:, cut], vis_r.at[k])
        push(near.at[:, cut], far.at[:, cut], far_s.at[k], far_r.at[k], other)
    for k in range(CHUNKS):
        arrived(sib.at[:, k * WIDE:(k + 1) * WIDE], sib_r.at[k])
    terms(1, sib)
    terms(2, near)
    for k in range(CHUNKS):
        arrived(far.at[:, k * WIDE:(k + 1) * WIDE], far_r.at[k])
    terms(3, far)

    def dense(q, carry):
        at = pl.ds(pl.multiple_of(q * 256, 256), 256)
        value = jnp.dot(mine[at, :], tlow[0:512, :], preferred_element_type=F32)
        value += jnp.dot(sib[at, :], tlow[512:1024, :], preferred_element_type=F32)
        value += jnp.dot(near[at, :], tlow[1024:1536, :], preferred_element_type=F32)
        value += jnp.dot(far[at, :], tlow[1536:2048, :], preferred_element_type=F32)
        for t in range(4):
            rows[pl.ds(q * 1024 + t, 256, stride=4), :] = value[:, t * 128:(t + 1) * 128]
        lines = pl.ds(pl.multiple_of(q * 1024, 1024), 1024)
        pltpu.make_async_copy(rows.at[lines, :], out_hbm.at[lines, :], out_s).start()
        return carry

    lax.fori_loop(0, 8, dense, 0)

    lane = lax.broadcasted_iota(jnp.int32, (1, VISITS), 1)
    listed = jnp.zeros((1, VISITS), F32)
    for s in range(VISITS):
        listed = jnp.where(lane == s, energies[s], listed)
    energy_out[...] = listed

    for copy in sends:
        copy.wait_send()
    pltpu.make_async_copy(rows, out_hbm, out_s).wait()


def local(raw_ints, metric, occ_energy, virt_energy):
    dma = pltpu.SemaphoreType.DMA
    vmem = pl.BlockSpec(memory_space=pltpu.VMEM)
    hbm = pl.BlockSpec(memory_space=pl.ANY)
    density, energy = pl.pallas_call(
        kernel,
        out_shape=(
            jax.ShapeDtypeStruct((NAUX * NV // 128, 128), F32),
            jax.ShapeDtypeStruct((1, VISITS), F32),
        ),
        in_specs=[vmem, hbm, pl.BlockSpec(memory_space=pltpu.SMEM), vmem],
        out_specs=(hbm, vmem),
        scratch_shapes=[
            pltpu.VMEM((16, 128, NV), BF16),
            pltpu.VMEM((NAUX, NV), BF16),
            pltpu.VMEM((NAUX, NAUX), BF16),
            pltpu.VMEM((NAUX, NV), BF16),
            pltpu.VMEM((NAUX, NV), BF16),
            pltpu.VMEM((NAUX, NV), BF16),
            pltpu.VMEM((NAUX, NV), BF16),
            pltpu.VMEM((NV, NAUX), BF16),
            pltpu.VMEM((NV, NV), F32),
            pltpu.VMEM((NV, NV), F32),
            pltpu.VMEM((NV, NV), F32),
            pltpu.VMEM((VISITS * NV, NV), BF16),
            pltpu.VMEM((NAUX * NV // 128, 128), F32),
            dma((CHUNKS, 16)), dma((CHUNKS,)),
            dma((8,)), dma(()),
            dma((4,)), dma((4,)),
            dma((4,)), dma((4,)),
            dma((4, 4)), dma((4,)),
            dma((4, 4)), dma((4,)),
            dma((4,)), dma(()),
            dma((CHUNKS,)), dma((CHUNKS,)),
            dma((CHUNKS,)), dma((CHUNKS,)),
            dma((CHUNKS,)), dma((CHUNKS,)),
            dma(()),
        ],
        compiler_params=pltpu.CompilerParams(
            collective_id=0, has_side_effects=True, vmem_limit_bytes=56 << 20
        ),
        name="pair_rows",
    )(raw_ints.reshape(NAUX, NV), metric, occ_energy, virt_energy.reshape(1, NV))
    return density.reshape(NAUX, 1, NV), energy


def solution(mesh):
    in_specs = (P("grp", "blk", None), P(None, "grp"), P(), P())
    out_specs = (P(None, ("blk", "grp"), None), P(("blk", "grp"), None))
    return jax.shard_map(local, mesh=mesh, in_specs=in_specs, out_specs=out_specs, check_vma=False)
```

```python
import jax
import jax.numpy as jnp
from jax import lax
from jax.experimental import pallas as pl
from jax.experimental.pallas import tpu as pltpu
from jax.sharding import PartitionSpec as P

VISITS = 4
NAUX = 2048
NV = 512
CUTS = ((0, 256), (256, 128), (384, 128))
SLOT = 72
MESH = pl.DeviceIdType.MESH
F32 = jnp.float32
BF16 = jnp.bfloat16


def device(xl, z, xh, y, c):
    return (xl * 8 + z, xh * 8 + y * 2 + c)


def pair_kernel(
    raw, metric, occ, virt, mine_out, sib_out, near_out, far_out, tlow_out, energy_out,
    send, owned, slots, full, mine, sib, near, far, mine_t, coul, amp, vsum, tlow,
    a2a_s, a2a_r, m1_s, m1_r, mx_s, mx_r, up_s, up_r, down_s, down_r, relay_s, relay_r,
    sw_s, sw_r, sib_s, sib_r, vis_s, vis_r, far_s, far_r, out_s,
):
    g = lax.axis_index("grp")
    b = lax.axis_index("blk")
    xl, z = g // 8, g % 8
    xh, y, c = b // 8, (b // 2) % 4, b % 2
    x = xh * 2 + xl
    other = (g, b + 1 - 2 * c)
    chip = g * 8 + xh * 4 + y
    ahead = (chip + 1 - 2 * c + 128) % 128
    behind = (chip + 127 + 2 * c) % 128

    def chip_core(n):
        return (n // 8, (n % 8) * 2 + c)

    def at_x(d):
        x2 = (x + d) % 4
        return device(x2 % 2, z, x2 // 2, y, c)

    def at_y(d):
        return device(xl, z, xh, (y + d) % 4, c)

    def at_g(d):
        return ((g + d) % 16, b)

    def at_z(d):
        return (xl * 8 + (z + d) % 8, b)

    barrier = pltpu.get_barrier_semaphore()
    partners = [at_g(d) for d in range(1, 16)]
    partners += [at_x(d) for d in range(1, 4)] + [at_y(d) for d in range(1, 4)]
    partners += [other, chip_core(ahead), chip_core(behind)]
    for partner in partners:
        pl.semaphore_signal(barrier, inc=1, device_id=partner, device_id_type=MESH)

    order = lax.broadcasted_iota(jnp.int32, (256, 256), 0)
    column = lax.broadcasted_iota(jnp.int32, (256, 256), 1)
    swap = jnp.where(column == (order % 16) * 16 + order // 16, 1.0, 0.0).astype(BF16)

    def relayout(k, carry):
        at = pl.multiple_of(k * 256, 256)
        moved = jnp.dot(swap, raw[pl.ds(at, 256), :], preferred_element_type=F32).astype(BF16)
        to = pl.multiple_of(k * 16, 16)
        for i in range(16):
            send[i, pl.ds(to, 16), :] = moved[i * 16:(i + 1) * 16, :]
        return carry

    lax.fori_loop(0, 8, relayout, 0)

    pl.semaphore_wait(barrier, len(partners))

    sends = []

    def push(src, dst, ssem, rsem, to):
        copy = pltpu.make_async_remote_copy(
            src_ref=src, dst_ref=dst, send_sem=ssem, recv_sem=rsem,
            device_id=to, device_id_type=MESH,
        )
        copy.start()
        sends.append(copy)

    def arrived(ref, sem):
        pltpu.make_async_copy(ref, ref, sem).wait()

    t = c * 8 + y * 2 + xh
    mine_columns = pl.ds(pl.multiple_of(g * 128, 128), 128)
    main_rows = pl.ds(pl.multiple_of((g * 128 + t * 64) % 2048, 64), 64)
    last_rows = pl.ds(pl.multiple_of((g * 128 + 1024 + t * 8) % 2048, 8), 8)
    parts = (
        (metric.at[main_rows, :], slots.at[t, pl.ds(0, 64), mine_columns]),
        (metric.at[last_rows, :], slots.at[t, pl.ds(64, 8), mine_columns]),
    )
    for d in (4, 3, 5, 2, 6, 1, 7):
        for h, (src, dst) in enumerate(parts):
            push(src, dst, m1_s.at[d, h], m1_r, at_z(d))
    for src, dst in parts:
        pltpu.make_async_copy(src, dst, m1_r).start()

    land = pl.ds(pl.multiple_of(g * 128, 128), 128)
    for k, (lo, wide) in enumerate(CUTS):
        cut = pl.ds(lo, wide)
        pltpu.make_async_copy(send.at[g, :, cut], owned.at[land, cut], a2a_r.at[k]).start()
        for d in range(1, 16):
            to = at_g(d)
            push(send.at[to[0], :, cut], owned.at[land, cut], a2a_s.at[k, d], a2a_r.at[k], to)

    def piece(py, e):
        px = (x + 4 - e) % 4
        at = c * 8 + py * 2 + px // 2
        return slots.at[at, :, pl.ds(pl.multiple_of((px % 2) * 1024, 1024), 1024)]

    below, above = (y + 3) % 4, (y + 1) % 4

    def spread(e):
        p = piece(y, e)
        push(p, p, up_s.at[e], up_r.at[e], at_y(1))
        push(p, p, down_s.at[e], down_r.at[e], at_y(3))

    def hand_over(py, k):
        p = slots.at[pl.ds(c * 8 + py * 2, 2), :, :]
        push(p, p, sw_s.at[k], sw_r, other)

    def relay_up(e):
        p = piece(below, e)
        arrived(p, up_r.at[e])
        push(p, p, relay_s.at[e], relay_r.at[e], at_y(1))

    def relay_down(e):
        p = piece(above, e)
        arrived(p, down_r.at[e])
        push(p, p, relay_s.at[e], relay_r.at[e], at_y(3))

    arrived(slots.at[t, :, pl.ds(0, 1024)], m1_r)
    for d in (1, 3, 2):
        push(piece(y, 0), piece(y, 0), mx_s.at[d], mx_r.at[d], at_x(d))
    spread(0)
    arrived(piece(y, 1), mx_r.at[1])
    spread(1)
    relay_up(0)
    arrived(piece(y, 3), mx_r.at[3])
    spread(3)
    relay_up(1)
    arrived(piece(y, 2), mx_r.at[2])
    spread(2)
    hand_over(y, 0)
    relay_down(3)
    arrived(piece(below, 3), up_r.at[3])
    arrived(piece(above, 0), down_r.at[0])
    arrived(piece(above, 1), down_r.at[1])
    relay_down(2)
    hand_over(above, 1)
    arrived(piece(below, 2), up_r.at[2])
    hand_over(below, 2)
    opposite = (y + 2) % 4
    for e in (0, 1, 3, 2):
        arrived(piece(opposite, e), relay_r.at[e])
    hand_over(opposite, 3)

    broad = jnp.broadcast_to(virt[...], (NV, NV))
    vsum[...] = broad + broad.T

    arrived(slots.at[pl.ds(0, 8), :, :], sw_r)

    def unfold(j, carry):
        column = pl.ds(pl.multiple_of(j * 128, 128), 128)

        def block(d, carry):
            i = (j + d) % 16
            row = pl.ds(pl.multiple_of(i * 128, 128), 128)
            value = slots[pl.ds(2 * d, 2), 0:64, column].reshape(128, 128)
            full[row, column] = value
            full[column, row] = value.T
            return carry

        lax.fori_loop(0, 8, block, 0, unroll=True)
        row = pl.ds(pl.multiple_of(((j + 8) % 16) * 128, 128), 128)
        value = slots[:, 64:72, column].astype(F32).reshape(128, 128)
        full[row, column] = value.astype(BF16)
        return carry

    lax.fori_loop(0, 16, unfold, 0)

    stores = []

    def keep(src, dst, n):
        copy = pltpu.make_async_copy(src, dst, out_s.at[n])
        copy.start()
        stores.append(copy)

    def visitor(k):
        cut = pl.ds(*CUTS[k])
        arrived(near.at[:, cut], vis_r.at[k])
        push(near.at[:, cut], far.at[:, cut], far_s.at[k], far_r.at[k], other)

    for k, (lo, wide) in enumerate(CUTS):
        cut = pl.ds(lo, wide)
        arrived(owned.at[:, cut], a2a_r.at[k])

        def fit(q, carry, cut=cut):
            at = pl.ds(pl.multiple_of(q * 1024, 1024), 1024)
            mine[at, cut] = jnp.dot(
                full[at, :], owned[:, cut], preferred_element_type=F32
            ).astype(BF16)
            return carry

        lax.fori_loop(0, 2, fit, 0)
        push(mine.at[:, cut], near.at[:, cut], vis_s.at[k], vis_r.at[k], chip_core(ahead))
        push(mine.at[:, cut], sib.at[:, cut], sib_s.at[k], sib_r.at[k], other)

        def turn(q, carry, lo=lo, wide=wide):
            at = pl.ds(pl.multiple_of(q * 256, 256), 256)
            mine_t[pl.ds(lo, wide), at] = mine[at, pl.ds(lo, wide)].T
            return carry

        lax.fori_loop(0, 8, turn, 0)
        if k == 1:
            visitor(0)
    keep(mine, mine_out, 0)

    def orbital(p):
        return (p % 16) * 16 + p // 16

    place = g * 16 + b
    e_own = occ[orbital(place)]

    def partner(s):
        if s == 0:
            return place
        even = (place + 256 - s) % 2 == 0
        return jnp.where(even, place + 256 - s, place + s) % 256

    def product(s, fit_of, lo, wide):
        cut = pl.ds(lo, wide)
        e_sum = e_own + occ[orbital(partner(s))]
        value = jnp.dot(mine_t[...], fit_of[:, cut], preferred_element_type=F32)
        coul[s, :, cut] = value
        amp[s, :, cut] = value / (e_sum - vsum[:, cut])

    energies = []

    def finish(s):
        total = jnp.zeros((128, NV), F32)
        for r in range(4):
            at = pl.ds(r * 128, 128)
            straight = amp[s, at, :]
            turned = amp[s, :, at].T
            total = total + coul[s, at, :] * (2.0 * straight - turned)
            tlow[pl.ds(s * NV + r * 128, 128), :] = (2.0 * turned - straight).astype(BF16)
        energies.append(jnp.sum(total))
        rows = pl.ds(s * NV, NV)
        keep(tlow.at[rows, :], tlow_out.at[rows, :], 4 + s)

    product(0, mine, 0, NV)
    finish(0)
    visitor(1)
    for k, (lo, wide) in enumerate(CUTS):
        arrived(sib.at[:, pl.ds(lo, wide)], sib_r.at[k])
    keep(sib, sib_out, 1)
    product(1, sib, 0, NV)
    finish(1)
    for k in (0, 1):
        product(2, near, *CUTS[k])
    for k in (0, 1):
        arrived(far.at[:, pl.ds(*CUTS[k])], far_r.at[k])
        product(3, far, *CUTS[k])
    visitor(2)
    keep(near, near_out, 2)
    product(2, near, *CUTS[2])
    finish(2)
    arrived(far.at[:, pl.ds(*CUTS[2])], far_r.at[2])
    keep(far, far_out, 3)
    product(3, far, *CUTS[2])
    finish(3)

    lane = lax.broadcasted_iota(jnp.int32, (1, VISITS), 1)
    listed = jnp.zeros((1, VISITS), F32)
    for s in range(VISITS):
        listed = jnp.where(lane == s, energies[s], listed)
    energy_out[...] = listed

    for copy in sends:
        copy.wait_send()
    for copy in stores:
        copy.wait()


def density_kernel(mine, sib, near, far, tlow, energy, out, energy_out):
    value = jnp.dot(mine[...], tlow[0:512, :], preferred_element_type=F32)
    value += jnp.dot(sib[...], tlow[512:1024, :], preferred_element_type=F32)
    value += jnp.dot(near[...], tlow[1024:1536, :], preferred_element_type=F32)
    value += jnp.dot(far[...], tlow[1536:2048, :], preferred_element_type=F32)
    for n in range(4):
        out[pl.ds(n, value.shape[0], stride=4), :] = value[:, n * 128:(n + 1) * 128]
    energy_out[...] = energy[...]


def local(raw_ints, metric, occ_energy, virt_energy):
    dma = pltpu.SemaphoreType.DMA
    vmem = pl.BlockSpec(memory_space=pltpu.VMEM)
    hbm = pl.BlockSpec(memory_space=pl.ANY)
    n = len(CUTS)
    fits = jax.ShapeDtypeStruct((NAUX, NV), BF16)
    fitted = pltpu.VMEM((NAUX, NV), BF16)
    mine, sib, near, far, tlow, energy = pl.pallas_call(
        pair_kernel,
        out_shape=(
            fits, fits, fits, fits,
            jax.ShapeDtypeStruct((VISITS * NV, NV), BF16),
            jax.ShapeDtypeStruct((1, VISITS), F32),
        ),
        in_specs=[vmem, hbm, pl.BlockSpec(memory_space=pltpu.SMEM), vmem],
        out_specs=(hbm, hbm, hbm, hbm, hbm, vmem),
        scratch_shapes=[
            pltpu.VMEM((16, 128, NV), BF16),
            fitted,
            pltpu.VMEM((16, SLOT, NAUX), BF16),
            pltpu.VMEM((NAUX, NAUX), BF16),
            fitted, fitted, fitted, fitted,
            pltpu.VMEM((NV, NAUX), BF16),
            pltpu.VMEM((VISITS, NV, NV), F32),
            pltpu.VMEM((VISITS, NV, NV), F32),
            pltpu.VMEM((NV, NV), F32),
            pltpu.VMEM((VISITS * NV, NV), BF16),
            dma((n, 16)), dma((n,)),
            dma((8, 2)), dma(()),
            dma((4,)), dma((4,)),
            dma((4,)), dma((4,)),
            dma((4,)), dma((4,)),
            dma((4,)), dma((4,)),
            dma((4,)), dma(()),
            dma((n,)), dma((n,)),
            dma((n,)), dma((n,)),
            dma((n,)), dma((n,)),
            dma((8,)),
        ],
        compiler_params=pltpu.CompilerParams(
            collective_id=0, has_side_effects=True, vmem_limit_bytes=56 << 20
        ),
        name="pair_terms",
    )(raw_ints.reshape(NAUX, NV), metric, occ_energy, virt_energy.reshape(1, NV))

    rows = 512
    part = pl.BlockSpec((rows, NV), lambda q: (q, 0))
    small = pl.BlockSpec((1, VISITS), lambda q: (0, 0))
    density, energy = pl.pallas_call(
        density_kernel,
        grid=(NAUX // rows,),
        out_shape=(
            jax.ShapeDtypeStruct((NAUX * NV // 128, 128), F32),
            jax.ShapeDtypeStruct((1, VISITS), F32),
        ),
        in_specs=[part, part, part, part, pl.BlockSpec((NAUX, NV), lambda q: (0, 0)), small],
        out_specs=(pl.BlockSpec((rows * 4, 128), lambda q: (q, 0)), small),
        compiler_params=pltpu.CompilerParams(vmem_limit_bytes=60 << 20),
        name="density_rows",
    )(mine, sib, near, far, tlow, energy)
    return density.reshape(NAUX, 1, NV), energy


def solution(mesh):
    in_specs = (P("grp", "blk", None), P(None, "grp"), P(), P())
    out_specs = (P(None, ("blk", "grp"), None), P(("blk", "grp"), None))
    return jax.shard_map(local, mesh=mesh, in_specs=in_specs, out_specs=out_specs, check_vma=False)
```

```python
import jax
import jax.numpy as jnp
from jax import lax
from jax.experimental import pallas as pl
from jax.experimental.pallas import tpu as pltpu
from jax.sharding import PartitionSpec as P

VISITS = 4
NAUX = 2048
NV = 512
CUTS = ((0, 128), (128, 128), (256, 128), (384, 128))
LAST = len(CUTS) - 1
SLOT = 72
MESH = pl.DeviceIdType.MESH
F32 = jnp.float32
BF16 = jnp.bfloat16


def device(xl, z, xh, y, c):
    return (xl * 8 + z, xh * 8 + y * 2 + c)


def pair_kernel(
    raw, metric, occ, virt, near_out, far_out, tlow_out, half_out, energy_out,
    send, owned, near_raw, bounce, slots, full, mine, sib, near, far, mine_t, coul, amp, vsum, tlow, half,
    a2a_s, a2a_r, m1_s, m1_r, mx_s, mx_r, up_s, up_r, down_s, down_r, relay_s, relay_r,
    sw_s, sw_r, sib_s, sib_r, vis_s, vis_r, far_s, far_r, hop_s, hop_r, out_s,
):
    g = lax.axis_index("grp")
    b = lax.axis_index("blk")
    xl, z = g // 8, g % 8
    xh, y, c = b // 8, (b // 2) % 4, b % 2
    x = xh * 2 + xl
    other = (g, b + 1 - 2 * c)
    chip = g * 8 + xh * 4 + y
    ahead = (chip + 1 - 2 * c + 128) % 128
    behind = (chip + 127 + 2 * c) % 128

    def chip_core(n):
        return (n // 8, (n % 8) * 2 + c)

    spot = xh * 4 + y
    gate = 7 - 7 * c
    crossing = spot == gate
    landing = ((g + 17 - 2 * c) % 16, 15 * c)

    def at_spot(r):
        return (g, r * 2 + c)

    def at_x(d):
        x2 = (x + d) % 4
        return device(x2 % 2, z, x2 // 2, y, c)

    def at_y(d):
        return device(xl, z, xh, (y + d) % 4, c)

    def at_g(d):
        return ((g + d) % 16, b)

    def at_z(d):
        return (xl * 8 + (z + d) % 8, b)

    barrier = pltpu.get_barrier_semaphore()
    partners = [at_g(d) for d in range(1, 16)]
    partners += [at_x(d) for d in range(1, 4)] + [at_y(d) for d in range(1, 4)]
    partners += [other, chip_core(ahead), chip_core(behind)]
    for partner in partners:
        pl.semaphore_signal(barrier, inc=1, device_id=partner, device_id_type=MESH)

    @pl.when(jnp.logical_not(crossing))
    def _():
        pl.semaphore_signal(barrier, inc=1, device_id=at_spot(gate), device_id_type=MESH)

    @pl.when(spot == 7 * c)
    def _():
        for r in range(8):
            pl.semaphore_signal(
                barrier, inc=1, device_id=((g + 15 + 2 * c) % 16, r * 2 + c), device_id_type=MESH
            )

    order = lax.broadcasted_iota(jnp.int32, (256, 256), 0)
    column = lax.broadcasted_iota(jnp.int32, (256, 256), 1)
    swap = jnp.where(column == (order % 16) * 16 + order // 16, 1.0, 0.0).astype(BF16)

    def relayout(k, carry):
        at = pl.multiple_of(k * 256, 256)
        moved = jnp.dot(swap, raw[pl.ds(at, 256), :], preferred_element_type=F32).astype(BF16)
        to = pl.multiple_of(k * 16, 16)
        for i in range(16):
            send[i, pl.ds(to, 16), :] = moved[i * 16:(i + 1) * 16, :]
        return carry

    lax.fori_loop(0, 8, relayout, 0)

    pl.semaphore_wait(barrier, len(partners) + 1 + jnp.where(crossing, 7, 0))

    sends = []

    def launch(src, dst, ssem, rsem, to):
        copy = pltpu.make_async_remote_copy(
            src_ref=src, dst_ref=dst, send_sem=ssem, recv_sem=rsem,
            device_id=to, device_id_type=MESH,
        )
        copy.start()
        return copy

    def push(src, dst, ssem, rsem, to):
        sends.append(launch(src, dst, ssem, rsem, to))

    def arrived(ref, sem):
        pltpu.make_async_copy(ref, ref, sem).wait()

    t = c * 8 + y * 2 + xh
    mine_columns = pl.ds(pl.multiple_of(g * 128, 128), 128)
    main_rows = pl.ds(pl.multiple_of((g * 128 + t * 64) % 2048, 64), 64)
    last_rows = pl.ds(pl.multiple_of((g * 128 + 1024 + t * 8) % 2048, 8), 8)
    parts = (
        (metric.at[main_rows, :], slots.at[t, pl.ds(0, 64), mine_columns]),
        (metric.at[last_rows, :], slots.at[t, pl.ds(64, 8), mine_columns]),
    )
    for d in (4, 3, 5, 2, 6, 1, 7):
        for h, (src, dst) in enumerate(parts):
            push(src, dst, m1_s.at[d, h], m1_r, at_z(d))
    for src, dst in parts:
        pltpu.make_async_copy(src, dst, m1_r).start()

    land = pl.ds(pl.multiple_of(g * 128, 128), 128)
    for k, (lo, wide) in enumerate(CUTS):
        cut = pl.ds(lo, wide)
        dst = owned.at[land, cut]
        pltpu.make_async_copy(send.at[g, :, cut], dst, a2a_r.at[k]).start()
        for d in range(1, 16):
            to = at_g(d)
            push(send.at[to[0], :, cut], dst, a2a_s.at[k, d], a2a_r.at[k], to)

    def chunk(k, rows):
        cut = pl.ds(*CUTS[k])
        if k == 0:
            return owned.at[rows, cut], near_raw.at[rows, :]
        return mine.at[rows, cut], near.at[rows, cut]

    def eighth(r):
        return pl.ds(pl.multiple_of(r * 256, 256), 256)

    def forward(k):
        @pl.when(jnp.logical_not(crossing))
        def _():
            src, dst = chunk(k, pl.ds(0, NAUX))
            launch(src, dst, vis_s.at[k], vis_r.at[k], chip_core(ahead))

        @pl.when(crossing)
        def _():
            for n in range(1, 8):
                r = (gate + n) % 8
                src, _ = chunk(k, eighth(r))
                launch(src, bounce.at[k], vis_s.at[k], hop_r.at[k], at_spot(r))
            src, dst = chunk(k, eighth(gate))
            launch(src, dst, vis_s.at[k], vis_r.at[k], landing)

    def hop(k):
        @pl.when(jnp.logical_not(crossing))
        def _():
            arrived(bounce.at[k], hop_r.at[k])
            _, dst = chunk(k, eighth(spot))
            launch(bounce.at[k], dst, hop_s.at[k], vis_r.at[k], landing)

    def piece(py, e):
        px = (x + 4 - e) % 4
        at = c * 8 + py * 2 + px // 2
        return slots.at[at, :, pl.ds(pl.multiple_of((px % 2) * 1024, 1024), 1024)]

    below, above = (y + 3) % 4, (y + 1) % 4

    def spread(e):
        p = piece(y, e)
        push(p, p, up_s.at[e], up_r.at[e], at_y(1))
        push(p, p, down_s.at[e], down_r.at[e], at_y(3))

    def hand_over(py, k):
        p = slots.at[pl.ds(c * 8 + py * 2, 2), :, :]
        push(p, p, sw_s.at[k], sw_r, other)

    def relay_up(e):
        p = piece(below, e)
        arrived(p, up_r.at[e])
        push(p, p, relay_s.at[e], relay_r.at[e], at_y(1))

    def relay_down(e):
        p = piece(above, e)
        arrived(p, down_r.at[e])
        push(p, p, relay_s.at[e], relay_r.at[e], at_y(3))

    arrived(slots.at[t, :, pl.ds(0, 1024)], m1_r)
    for d in (1, 3, 2):
        push(piece(y, 0), piece(y, 0), mx_s.at[d], mx_r.at[d], at_x(d))
    spread(0)
    arrived(piece(y, 1), mx_r.at[1])
    spread(1)
    relay_up(0)
    arrived(piece(y, 3), mx_r.at[3])
    spread(3)
    relay_up(1)
    arrived(piece(y, 2), mx_r.at[2])
    spread(2)
    hand_over(y, 0)
    relay_down(3)
    arrived(piece(below, 3), up_r.at[3])
    arrived(piece(above, 0), down_r.at[0])
    arrived(piece(above, 1), down_r.at[1])
    relay_down(2)
    arrived(owned.at[:, pl.ds(*CUTS[0])], a2a_r.at[0])
    forward(0)
    hand_over(above, 1)
    arrived(piece(below, 2), up_r.at[2])
    hand_over(below, 2)
    hop(0)
    opposite = (y + 2) % 4
    for e in (0, 1, 3, 2):
        arrived(piece(opposite, e), relay_r.at[e])
    hand_over(opposite, 3)

    broad = jnp.broadcast_to(virt[...], (NV, NV))
    vsum[...] = broad + broad.T

    arrived(slots.at[pl.ds(0, 8), :, :], sw_r)

    def unfold(j, carry):
        column = pl.ds(pl.multiple_of(j * 128, 128), 128)

        def block(d, carry):
            i = (j + d) % 16
            row = pl.ds(pl.multiple_of(i * 128, 128), 128)
            value = slots[pl.ds(2 * d, 2), 0:64, column].reshape(128, 128)
            full[row, column] = value
            full[column, row] = value.T
            return carry

        lax.fori_loop(0, 8, block, 0, unroll=True)
        row = pl.ds(pl.multiple_of(((j + 8) % 16) * 128, 128), 128)
        value = slots[:, 64:72, column].astype(F32).reshape(128, 128)
        full[row, column] = value.astype(BF16)
        return carry

    lax.fori_loop(0, 16, unfold, 0)

    stores = []

    def keep(src, dst, n):
        copy = pltpu.make_async_copy(src, dst, out_s.at[n])
        copy.start()
        stores.append(copy)

    def share(src, dst, k, ssem, rsem):
        cut = pl.ds(*CUTS[k])
        push(src.at[:, cut], dst.at[:, cut], ssem.at[k], rsem.at[k], other)

    def fit(src, dst, first, size):
        cut = pl.ds(first, size)

        def step(q, carry):
            at = pl.ds(pl.multiple_of(q * 1024, 1024), 1024)
            dst[at, cut] = jnp.dot(
                full[at, :], src[:, cut], preferred_element_type=F32
            ).astype(BF16)
            return carry

        lax.fori_loop(0, 2, step, 0)

    def turn(first, size):
        def step(q, carry):
            at = pl.ds(pl.multiple_of(q * 256, 256), 256)
            mine_t[pl.ds(first, size), at] = mine[at, pl.ds(first, size)].T
            return carry

        lax.fori_loop(0, 8, step, 0)

    def visitor(k):
        _, dst = chunk(k, pl.ds(0, NAUX))
        arrived(dst, vis_r.at[k])
        if k == 0:
            fit(near_raw, near, 0, 128)
        share(near, far, k, far_s, far_r)

    arrived(owned.at[:, pl.ds(*CUTS[1])], a2a_r.at[1])
    fit(owned, mine, 0, 256)
    forward(1)
    share(mine, sib, 0, sib_s, sib_r)
    share(mine, sib, 1, sib_s, sib_r)
    turn(0, 256)
    hop(1)
    visitor(0)
    for k in (2, 3):
        lo, wide = CUTS[k]
        arrived(owned.at[:, pl.ds(lo, wide)], a2a_r.at[k])
        fit(owned, mine, lo, wide)
        forward(k)
        share(mine, sib, k, sib_s, sib_r)
        turn(lo, wide)
        hop(k)
        if k == 2:
            visitor(1)

    def orbital(p):
        return (p % 16) * 16 + p // 16

    place = g * 16 + b
    e_own = occ[orbital(place)]

    def partner(s):
        if s == 0:
            return place
        even = (place + 256 - s) % 2 == 0
        return jnp.where(even, place + 256 - s, place + s) % 256

    def product(s, fit_of, lo, wide):
        cut = pl.ds(lo, wide)
        e_sum = e_own + occ[orbital(partner(s))]
        value = jnp.dot(mine_t[...], fit_of[:, cut], preferred_element_type=F32)
        coul[s, :, cut] = value
        amp[s, :, cut] = value / (e_sum - vsum[:, cut])

    energies = []

    def finish(s):
        total = jnp.zeros((128, NV), F32)
        for r in range(4):
            at = pl.ds(r * 128, 128)
            straight = amp[s, at, :]
            turned = amp[s, :, at].T
            total = total + coul[s, at, :] * (2.0 * straight - turned)
            tlow[pl.ds(s * NV + r * 128, 128), :] = (2.0 * turned - straight).astype(BF16)
        energies.append(jnp.sum(total))
        if s >= 2:
            keep(tlow.at[pl.ds(s * NV, NV), :], tlow_out.at[pl.ds((s - 2) * NV, NV), :], 2 + s)

    product(0, mine, 0, NV)
    finish(0)
    visitor(2)
    for k in range(len(CUTS)):
        arrived(sib.at[:, pl.ds(*CUTS[k])], sib_r.at[k])
    product(1, sib, 0, NV)
    finish(1)

    def resident(q, carry):
        at = pl.ds(pl.multiple_of(q * 1024, 1024), 1024)
        value = jnp.dot(mine[at, :], tlow[0:512, :], preferred_element_type=F32)
        half[at, :] = value + jnp.dot(sib[at, :], tlow[512:1024, :], preferred_element_type=F32)
        return carry

    lax.fori_loop(0, 2, resident, 0)
    keep(half, half_out, 0)
    product(2, near, 0, 256)
    for k in range(LAST):
        arrived(far.at[:, pl.ds(*CUTS[k])], far_r.at[k])
    product(3, far, 0, 256)
    visitor(LAST)
    keep(near, near_out, 2)
    product(2, near, 256, 256)
    finish(2)
    arrived(far.at[:, pl.ds(*CUTS[LAST])], far_r.at[LAST])
    keep(far, far_out, 3)
    product(3, far, 256, 256)
    finish(3)

    lane = lax.broadcasted_iota(jnp.int32, (1, VISITS), 1)
    listed = jnp.zeros((1, VISITS), F32)
    for s in range(VISITS):
        listed = jnp.where(lane == s, energies[s], listed)
    energy_out[...] = listed

    for copy in sends:
        copy.wait_send()
    for k in range(len(CUTS)):
        arrived(mine.at[:, pl.ds(*CUTS[k])], vis_s.at[k])

        @pl.when(jnp.logical_not(crossing))
        def _():
            arrived(bounce.at[k], hop_s.at[k])

    for copy in stores:
        copy.wait()


def density_kernel(near, far, tlow, half, energy, out, energy_out):
    value = half[...] + jnp.dot(near[...], tlow[0:512, :], preferred_element_type=F32)
    value += jnp.dot(far[...], tlow[512:1024, :], preferred_element_type=F32)
    for n in range(4):
        out[pl.ds(n, value.shape[0], stride=4), :] = value[:, n * 128:(n + 1) * 128]
    energy_out[...] = energy[...]


def local(raw_ints, metric, occ_energy, virt_energy):
    dma = pltpu.SemaphoreType.DMA
    vmem = pl.BlockSpec(memory_space=pltpu.VMEM)
    hbm = pl.BlockSpec(memory_space=pl.ANY)
    n = len(CUTS)
    fits = jax.ShapeDtypeStruct((NAUX, NV), BF16)
    fitted = pltpu.VMEM((NAUX, NV), BF16)
    near, far, tlow, half, energy = pl.pallas_call(
        pair_kernel,
        out_shape=(
            fits, fits,
            jax.ShapeDtypeStruct((2 * NV, NV), BF16),
            jax.ShapeDtypeStruct((NAUX, NV), F32),
            jax.ShapeDtypeStruct((1, VISITS), F32),
        ),
        in_specs=[vmem, hbm, pl.BlockSpec(memory_space=pltpu.SMEM), vmem],
        out_specs=(hbm, hbm, hbm, hbm, vmem),
        scratch_shapes=[
            pltpu.VMEM((16, 128, NV), BF16),
            fitted,
            pltpu.VMEM((NAUX, 128), BF16),
            pltpu.VMEM((n, 256, 128), BF16),
            pltpu.VMEM((16, SLOT, NAUX), BF16),
            pltpu.VMEM((NAUX, NAUX), BF16),
            fitted, fitted, fitted, fitted,
            pltpu.VMEM((NV, NAUX), BF16),
            pltpu.VMEM((VISITS, NV, NV), F32),
            pltpu.VMEM((VISITS, NV, NV), F32),
            pltpu.VMEM((NV, NV), F32),
            pltpu.VMEM((VISITS * NV, NV), BF16),
            pltpu.VMEM((NAUX, NV), F32),
            dma((n, 16)), dma((n,)),
            dma((8, 2)), dma(()),
            dma((4,)), dma((4,)),
            dma((4,)), dma((4,)),
            dma((4,)), dma((4,)),
            dma((4,)), dma((4,)),
            dma((4,)), dma(()),
            dma((n,)), dma((n,)),
            dma((n,)), dma((n,)),
            dma((n,)), dma((n,)),
            dma((n,)), dma((n,)),
            dma((8,)),
        ],
        compiler_params=pltpu.CompilerParams(
            collective_id=0, has_side_effects=True, vmem_limit_bytes=56 << 20
        ),
        name="pair_terms",
    )(raw_ints.reshape(NAUX, NV), metric, occ_energy, virt_energy.reshape(1, NV))

    rows = 1024
    part = pl.BlockSpec((rows, NV), lambda q: (q, 0))
    small = pl.BlockSpec((1, VISITS), lambda q: (0, 0))
    density, energy = pl.pallas_call(
        density_kernel,
        grid=(NAUX // rows,),
        out_shape=(
            jax.ShapeDtypeStruct((NAUX * NV // 128, 128), F32),
            jax.ShapeDtypeStruct((1, VISITS), F32),
        ),
        in_specs=[part, part, pl.BlockSpec((2 * NV, NV), lambda q: (0, 0)), part, small],
        out_specs=(pl.BlockSpec((rows * 4, 128), lambda q: (q, 0)), small),
        compiler_params=pltpu.CompilerParams(vmem_limit_bytes=60 << 20),
        name="density_rows",
    )(near, far, tlow, half, energy)
    return density.reshape(NAUX, 1, NV), energy


def solution(mesh):
    in_specs = (P("grp", "blk", None), P(None, "grp"), P(), P())
    out_specs = (P(None, ("blk", "grp"), None), P(("blk", "grp"), None))
    return jax.shard_map(local, mesh=mesh, in_specs=in_specs, out_specs=out_specs, check_vma=False)
```

```python
import jax
import jax.numpy as jnp
from jax import lax
from jax.experimental import pallas as pl
from jax.experimental.pallas import tpu as pltpu
from jax.sharding import PartitionSpec as P

VISITS = 4
NAUX = 2048
NV = 512
CUTS = ((0, 128), (128, 128), (256, 128), (384, 128))
LAST = len(CUTS) - 1
SLOT = 72
MESH = pl.DeviceIdType.MESH
F32 = jnp.float32
BF16 = jnp.bfloat16


def device(xl, z, xh, y, c):
    return (xl * 8 + z, xh * 8 + y * 2 + c)


def pair_kernel(
    raw, metric, occ, virt, near_out, far_out, tlow_out, half_out, energy_out,
    send, owned, near_raw, bounce, slots, full, mine, sib, near, far, mine_t, coul, amp, vsum, tlow, half,
    a2a_s, a2a_r, m1_s, m1_r, mx_s, mx_r, up_s, up_r, down_s, down_r, relay_s, relay_r,
    sw_s, sw_r, sib_s, sib_r, vis_s, vis_r, far_s, far_r, hop_s, hop_r, out_s,
):
    g = lax.axis_index("grp")
    b = lax.axis_index("blk")
    xl, z = g // 8, g % 8
    xh, y, c = b // 8, (b // 2) % 4, b % 2
    x = xh * 2 + xl
    other = (g, b + 1 - 2 * c)
    chip = g * 8 + xh * 4 + y
    ahead = (chip + 1 - 2 * c + 128) % 128
    behind = (chip + 127 + 2 * c) % 128

    def chip_core(n):
        return (n // 8, (n % 8) * 2 + c)

    spot = xh * 4 + y
    gate = 7 - 7 * c
    crossing = spot == gate
    landing = ((g + 17 - 2 * c) % 16, 15 * c)

    def at_spot(r):
        return (g, r * 2 + c)

    def at_x(d):
        x2 = (x + d) % 4
        return device(x2 % 2, z, x2 // 2, y, c)

    def at_y(d):
        return device(xl, z, xh, (y + d) % 4, c)

    def at_g(d):
        return ((g + d) % 16, b)

    def at_z(d):
        return (xl * 8 + (z + d) % 8, b)

    barrier = pltpu.get_barrier_semaphore()
    partners = [at_g(d) for d in range(1, 16)]
    partners += [at_x(d) for d in range(1, 4)] + [at_y(d) for d in range(1, 4)]
    partners += [other, chip_core(ahead), chip_core(behind)]
    for partner in partners:
        pl.semaphore_signal(barrier, inc=1, device_id=partner, device_id_type=MESH)

    @pl.when(jnp.logical_not(crossing))
    def _():
        pl.semaphore_signal(barrier, inc=1, device_id=at_spot(gate), device_id_type=MESH)

    @pl.when(spot == 7 * c)
    def _():
        for r in range(8):
            pl.semaphore_signal(
                barrier, inc=1, device_id=((g + 15 + 2 * c) % 16, r * 2 + c), device_id_type=MESH
            )

    order = lax.broadcasted_iota(jnp.int32, (256, 256), 0)
    column = lax.broadcasted_iota(jnp.int32, (256, 256), 1)
    swap = jnp.where(column == (order % 16) * 16 + order // 16, 1.0, 0.0).astype(BF16)

    def relayout(k, carry):
        at = pl.multiple_of(k * 256, 256)
        moved = jnp.dot(swap, raw[pl.ds(at, 256), :], preferred_element_type=F32).astype(BF16)
        to = pl.multiple_of(k * 16, 16)
        for i in range(16):
            send[i, pl.ds(to, 16), :] = moved[i * 16:(i + 1) * 16, :]
        return carry

    lax.fori_loop(0, 8, relayout, 0)

    pl.semaphore_wait(barrier, len(partners) + 1 + jnp.where(crossing, 7, 0))

    sends = []

    def launch(src, dst, ssem, rsem, to):
        copy = pltpu.make_async_remote_copy(
            src_ref=src, dst_ref=dst, send_sem=ssem, recv_sem=rsem,
            device_id=to, device_id_type=MESH,
        )
        copy.start()
        return copy

    def push(src, dst, ssem, rsem, to):
        sends.append(launch(src, dst, ssem, rsem, to))

    def arrived(ref, sem):
        pltpu.make_async_copy(ref, ref, sem).wait()

    t = c * 8 + y * 2 + xh
    mine_columns = pl.ds(pl.multiple_of(g * 128, 128), 128)
    main_rows = pl.ds(pl.multiple_of((g * 128 + t * 64) % 2048, 64), 64)
    last_rows = pl.ds(pl.multiple_of((g * 128 + 1024 + t * 8) % 2048, 8), 8)
    parts = (
        (metric.at[main_rows, :], slots.at[t, pl.ds(0, 64), mine_columns]),
        (metric.at[last_rows, :], slots.at[t, pl.ds(64, 8), mine_columns]),
    )
    for d in (4, 3, 5, 2, 6, 1, 7):
        for h, (src, dst) in enumerate(parts):
            push(src, dst, m1_s.at[d, h], m1_r, at_z(d))
    for src, dst in parts:
        pltpu.make_async_copy(src, dst, m1_r).start()

    land = pl.ds(pl.multiple_of(g * 128, 128), 128)
    for k, (lo, wide) in enumerate(CUTS):
        cut = pl.ds(lo, wide)
        dst = owned.at[land, cut]
        pltpu.make_async_copy(send.at[g, :, cut], dst, a2a_r.at[k]).start()
        for d in range(1, 16):
            to = at_g(d)
            push(send.at[to[0], :, cut], dst, a2a_s.at[k, d], a2a_r.at[k], to)

    def chunk(k, rows):
        cut = pl.ds(*CUTS[k])
        if k == 0:
            return owned.at[rows, cut], near_raw.at[rows, :]
        return mine.at[rows, cut], near.at[rows, cut]

    def eighth(r):
        return pl.ds(pl.multiple_of(r * 256, 256), 256)

    def forward(k):
        @pl.when(jnp.logical_not(crossing))
        def _():
            src, dst = chunk(k, pl.ds(0, NAUX))
            launch(src, dst, vis_s.at[k], vis_r.at[k], chip_core(ahead))

        @pl.when(crossing)
        def _():
            for n in range(1, 8):
                r = (gate + n) % 8
                src, _ = chunk(k, eighth(r))
                launch(src, bounce.at[k], vis_s.at[k], hop_r.at[k], at_spot(r))
            src, dst = chunk(k, eighth(gate))
            launch(src, dst, vis_s.at[k], vis_r.at[k], landing)

    def forward_half(k, h):
        @pl.when(jnp.logical_not(crossing))
        def _():
            src, dst = chunk(k, pl.ds(h * 1024, 1024))
            launch(src, dst, vis_s.at[k], vis_r.at[k], chip_core(ahead))

        for r in range(4 * h, 4 * h + 4):
            @pl.when(jnp.logical_and(crossing, r != gate))
            def _():
                src, _ = chunk(k, eighth(r))
                launch(src, bounce.at[k], vis_s.at[k], hop_r.at[k], at_spot(r))

            @pl.when(jnp.logical_and(crossing, r == gate))
            def _():
                src, dst = chunk(k, eighth(r))
                launch(src, dst, vis_s.at[k], vis_r.at[k], landing)

    def hop(k):
        @pl.when(jnp.logical_not(crossing))
        def _():
            arrived(bounce.at[k], hop_r.at[k])
            _, dst = chunk(k, eighth(spot))
            launch(bounce.at[k], dst, hop_s.at[k], vis_r.at[k], landing)

    def piece(py, e):
        px = (x + 4 - e) % 4
        at = c * 8 + py * 2 + px // 2
        return slots.at[at, :, pl.ds(pl.multiple_of((px % 2) * 1024, 1024), 1024)]

    below, above = (y + 3) % 4, (y + 1) % 4

    def spread(e):
        p = piece(y, e)
        push(p, p, up_s.at[e], up_r.at[e], at_y(1))
        push(p, p, down_s.at[e], down_r.at[e], at_y(3))

    def hand_over(py, k):
        p = slots.at[pl.ds(c * 8 + py * 2, 2), :, :]
        push(p, p, sw_s.at[k], sw_r, other)

    def relay_up(e):
        p = piece(below, e)
        arrived(p, up_r.at[e])
        push(p, p, relay_s.at[e], relay_r.at[e], at_y(1))

    def relay_down(e):
        p = piece(above, e)
        arrived(p, down_r.at[e])
        push(p, p, relay_s.at[e], relay_r.at[e], at_y(3))

    arrived(slots.at[t, :, pl.ds(0, 1024)], m1_r)
    for d in (1, 3, 2):
        push(piece(y, 0), piece(y, 0), mx_s.at[d], mx_r.at[d], at_x(d))
    spread(0)
    arrived(piece(y, 1), mx_r.at[1])
    spread(1)
    relay_up(0)
    arrived(piece(y, 3), mx_r.at[3])
    spread(3)
    relay_up(1)
    arrived(piece(y, 2), mx_r.at[2])
    spread(2)
    hand_over(y, 0)
    relay_down(3)
    arrived(piece(below, 3), up_r.at[3])
    arrived(piece(above, 0), down_r.at[0])
    arrived(piece(above, 1), down_r.at[1])
    relay_down(2)
    hand_over(above, 1)
    arrived(piece(below, 2), up_r.at[2])
    hand_over(below, 2)
    opposite = (y + 2) % 4
    for e in (0, 1, 3, 2):
        arrived(piece(opposite, e), relay_r.at[e])
    hand_over(opposite, 3)
    arrived(owned.at[:, pl.ds(*CUTS[0])], a2a_r.at[0])
    forward(0)
    hop(0)

    broad = jnp.broadcast_to(virt[...], (NV, NV))
    vsum[...] = broad + broad.T

    arrived(slots.at[pl.ds(0, 8), :, :], sw_r)

    def unfold(j, carry):
        column = pl.ds(pl.multiple_of(j * 128, 128), 128)

        def block(d, carry):
            i = (j + d) % 16
            row = pl.ds(pl.multiple_of(i * 128, 128), 128)
            value = slots[pl.ds(2 * d, 2), 0:64, column].reshape(128, 128)
            full[row, column] = value
            full[column, row] = value.T
            return carry

        lax.fori_loop(0, 8, block, 0, unroll=True)
        row = pl.ds(pl.multiple_of(((j + 8) % 16) * 128, 128), 128)
        value = slots[:, 64:72, column].astype(F32).reshape(128, 128)
        full[row, column] = value.astype(BF16)
        return carry

    lax.fori_loop(0, 16, unfold, 0)

    stores = []

    def keep(src, dst, n):
        copy = pltpu.make_async_copy(src, dst, out_s.at[n])
        copy.start()
        stores.append(copy)

    def share(src, dst, k, ssem, rsem):
        cut = pl.ds(*CUTS[k])
        push(src.at[:, cut], dst.at[:, cut], ssem.at[k], rsem.at[k], other)

    def fit(src, dst, first, size):
        cut = pl.ds(first, size)

        def step(q, carry):
            at = pl.ds(pl.multiple_of(q * 1024, 1024), 1024)
            dst[at, cut] = jnp.dot(
                full[at, :], src[:, cut], preferred_element_type=F32
            ).astype(BF16)
            return carry

        lax.fori_loop(0, 2, step, 0)

    def fit_and_send(k, first, size):
        cut = pl.ds(first, size)
        for h in range(2):
            at = pl.ds(h * 1024, 1024)
            mine[at, cut] = jnp.dot(
                full[at, :], owned[:, cut], preferred_element_type=F32
            ).astype(BF16)
            forward_half(k, h)

    def turn(first, size):
        def step(q, carry):
            at = pl.ds(pl.multiple_of(q * 256, 256), 256)
            mine_t[pl.ds(first, size), at] = mine[at, pl.ds(first, size)].T
            return carry

        lax.fori_loop(0, 8, step, 0)

    def visitor(k):
        _, dst = chunk(k, pl.ds(0, NAUX))
        arrived(dst, vis_r.at[k])
        if k == 0:
            fit(near_raw, near, 0, 128)
        share(near, far, k, far_s, far_r)

    arrived(owned.at[:, pl.ds(*CUTS[1])], a2a_r.at[1])
    fit_and_send(1, 0, 256)
    share(mine, sib, 0, sib_s, sib_r)
    share(mine, sib, 1, sib_s, sib_r)
    turn(0, 256)
    hop(1)
    visitor(0)
    for k in (2, 3):
        lo, wide = CUTS[k]
        arrived(owned.at[:, pl.ds(lo, wide)], a2a_r.at[k])
        fit_and_send(k, lo, wide)
        share(mine, sib, k, sib_s, sib_r)
        turn(lo, wide)
        hop(k)
        if k == 2:
            visitor(1)

    def orbital(p):
        return (p % 16) * 16 + p // 16

    place = g * 16 + b
    e_own = occ[orbital(place)]

    def partner(s):
        if s == 0:
            return place
        even = (place + 256 - s) % 2 == 0
        return jnp.where(even, place + 256 - s, place + s) % 256

    def product(s, fit_of, lo, wide):
        cut = pl.ds(lo, wide)
        e_sum = e_own + occ[orbital(partner(s))]
        value = jnp.dot(mine_t[...], fit_of[:, cut], preferred_element_type=F32)
        coul[s, :, cut] = value
        amp[s, :, cut] = value / (e_sum - vsum[:, cut])

    energies = []

    def finish(s):
        total = jnp.zeros((128, NV), F32)
        for r in range(4):
            at = pl.ds(r * 128, 128)
            straight = amp[s, at, :]
            turned = amp[s, :, at].T
            total = total + coul[s, at, :] * (2.0 * straight - turned)
            tlow[pl.ds(s * NV + r * 128, 128), :] = (2.0 * turned - straight).astype(BF16)
        energies.append(jnp.sum(total))
        if s >= 2:
            keep(tlow.at[pl.ds(s * NV, NV), :], tlow_out.at[pl.ds((s - 2) * NV, NV), :], 2 + s)

    product(0, mine, 0, NV)
    finish(0)
    visitor(2)
    for k in range(len(CUTS)):
        arrived(sib.at[:, pl.ds(*CUTS[k])], sib_r.at[k])
    product(1, sib, 0, NV)
    finish(1)

    def resident(q, carry):
        at = pl.ds(pl.multiple_of(q * 1024, 1024), 1024)
        value = jnp.dot(mine[at, :], tlow[0:512, :], preferred_element_type=F32)
        half[at, :] = value + jnp.dot(sib[at, :], tlow[512:1024, :], preferred_element_type=F32)
        return carry

    lax.fori_loop(0, 2, resident, 0)
    keep(half, half_out, 0)
    product(2, near, 0, 256)
    for k in range(LAST):
        arrived(far.at[:, pl.ds(*CUTS[k])], far_r.at[k])
    product(3, far, 0, 256)
    visitor(LAST)
    keep(near, near_out, 2)
    product(2, near, 256, 256)
    finish(2)
    arrived(far.at[:, pl.ds(*CUTS[LAST])], far_r.at[LAST])
    keep(far, far_out, 3)
    product(3, far, 256, 256)
    finish(3)

    lane = lax.broadcasted_iota(jnp.int32, (1, VISITS), 1)
    listed = jnp.zeros((1, VISITS), F32)
    for s in range(VISITS):
        listed = jnp.where(lane == s, energies[s], listed)
    energy_out[...] = listed

    for copy in sends:
        copy.wait_send()
    for k in range(len(CUTS)):
        arrived(mine.at[:, pl.ds(*CUTS[k])], vis_s.at[k])

        @pl.when(jnp.logical_not(crossing))
        def _():
            arrived(bounce.at[k], hop_s.at[k])

    for copy in stores:
        copy.wait()


def density_kernel(near, far, tlow, half, energy, out, energy_out):
    value = half[...] + jnp.dot(near[...], tlow[0:512, :], preferred_element_type=F32)
    value += jnp.dot(far[...], tlow[512:1024, :], preferred_element_type=F32)
    for n in range(4):
        out[pl.ds(n, value.shape[0], stride=4), :] = value[:, n * 128:(n + 1) * 128]
    energy_out[...] = energy[...]


def local(raw_ints, metric, occ_energy, virt_energy):
    dma = pltpu.SemaphoreType.DMA
    vmem = pl.BlockSpec(memory_space=pltpu.VMEM)
    hbm = pl.BlockSpec(memory_space=pl.ANY)
    n = len(CUTS)
    fits = jax.ShapeDtypeStruct((NAUX, NV), BF16)
    fitted = pltpu.VMEM((NAUX, NV), BF16)
    near, far, tlow, half, energy = pl.pallas_call(
        pair_kernel,
        out_shape=(
            fits, fits,
            jax.ShapeDtypeStruct((2 * NV, NV), BF16),
            jax.ShapeDtypeStruct((NAUX, NV), F32),
            jax.ShapeDtypeStruct((1, VISITS), F32),
        ),
        in_specs=[vmem, hbm, pl.BlockSpec(memory_space=pltpu.SMEM), vmem],
        out_specs=(hbm, hbm, hbm, hbm, vmem),
        scratch_shapes=[
            pltpu.VMEM((16, 128, NV), BF16),
            fitted,
            pltpu.VMEM((NAUX, 128), BF16),
            pltpu.VMEM((n, 256, 128), BF16),
            pltpu.VMEM((16, SLOT, NAUX), BF16),
            pltpu.VMEM((NAUX, NAUX), BF16),
            fitted, fitted, fitted, fitted,
            pltpu.VMEM((NV, NAUX), BF16),
            pltpu.VMEM((VISITS, NV, NV), F32),
            pltpu.VMEM((VISITS, NV, NV), F32),
            pltpu.VMEM((NV, NV), F32),
            pltpu.VMEM((VISITS * NV, NV), BF16),
            pltpu.VMEM((NAUX, NV), F32),
            dma((n, 16)), dma((n,)),
            dma((8, 2)), dma(()),
            dma((4,)), dma((4,)),
            dma((4,)), dma((4,)),
            dma((4,)), dma((4,)),
            dma((4,)), dma((4,)),
            dma((4,)), dma(()),
            dma((n,)), dma((n,)),
            dma((n,)), dma((n,)),
            dma((n,)), dma((n,)),
            dma((n,)), dma((n,)),
            dma((8,)),
        ],
        compiler_params=pltpu.CompilerParams(
            collective_id=0, has_side_effects=True, vmem_limit_bytes=56 << 20
        ),
        name="pair_terms",
    )(raw_ints.reshape(NAUX, NV), metric, occ_energy, virt_energy.reshape(1, NV))

    rows = 1024
    part = pl.BlockSpec((rows, NV), lambda q: (q, 0))
    small = pl.BlockSpec((1, VISITS), lambda q: (0, 0))
    density, energy = pl.pallas_call(
        density_kernel,
        grid=(NAUX // rows,),
        out_shape=(
            jax.ShapeDtypeStruct((NAUX * NV // 128, 128), F32),
            jax.ShapeDtypeStruct((1, VISITS), F32),
        ),
        in_specs=[part, part, pl.BlockSpec((2 * NV, NV), lambda q: (0, 0)), part, small],
        out_specs=(pl.BlockSpec((rows * 4, 128), lambda q: (q, 0)), small),
        compiler_params=pltpu.CompilerParams(vmem_limit_bytes=60 << 20),
        name="density_rows",
    )(near, far, tlow, half, energy)
    return density.reshape(NAUX, 1, NV), energy


def solution(mesh):
    in_specs = (P("grp", "blk", None), P(None, "grp"), P(), P())
    out_specs = (P(None, ("blk", "grp"), None), P(("blk", "grp"), None))
    return jax.shard_map(local, mesh=mesh, in_specs=in_specs, out_specs=out_specs, check_vma=False)
```
